32 devices in a mesh: ep: 8 (over z, x), tp: 4 (over y, core).
Axes of the slice: x: 2, y: 2, z: 4, core: 2. Of those that a mesh axis runs over, the one named last changes fastest.
Arguments:
- tokens: bfloat16 [2, 1024, 4096], P(None, 'ep', 'tp'), may hold values from -6 to 6
- expert_ids: int32 [2, 1024, 8], P(None, 'ep'), may hold values from 0 to 31, all different within a row; in each aligned block of 128 rows (0 to 127, 128 to 255, ..., all dimensions but the last counted through in order) at most 40 rows name the same one
- route_weight: float32 [2, 1024, 8], P(None, 'ep'), may hold values from 0.1 to 1
- gate_weight: bfloat16 [32, 1536, 4096], P('ep', 'tp'), may hold values from -0.09375 to 0.09375
- up_weight: bfloat16 [32, 1536, 4096], P('ep', 'tp'), may hold values from -0.09375 to 0.09375
- down_weight: bfloat16 [32, 1536, 4096], P('ep', None, 'tp'), may hold values from -0.15625 to 0.15625
- home_slot: int32 [32], replicated, may hold values from 0 to 31, as said below
- spare_expert: int32 [8], replicated, may hold values from 0 to 31, as said below
Outputs:
- mixed: bfloat16 [2, 1024, 4096], P(None, 'ep', 'tp')
- spare_gate: bfloat16 [8, 1536, 4096], P('ep', 'tp')
- spare_up: bfloat16 [8, 1536, 4096], P('ep', 'tp')
- spare_down: bfloat16 [8, 1536, 4096], P('ep', None, 'tp')
The draws below stay inside these ranges and needn't reach their ends.
Inputs may be any that keep to these rules, and one draw needn't show every extreme that they name: `home_slot`: a permutation; slot s belongs to ep index s // 4. `spare_expert`: names at most 6 distinct experts, whose home slots lie on distinct ep indices; entry d never names an expert whose home slot lies on ep index d. `expert_ids`: each token names 8 distinct experts; in each micro-step the 128 tokens of one ep index name one expert at most 40 times.
All inputs are finite; a program needn't handle non-finite values.
Results may differ from the reference program's by a relative error of at most 0.0058.
Values may be sent and summed in bfloat16 or wider, within the bound.
No kernel may reach another device: no remote copies, remote signals or barrier semaphores. Data moves between devices by JAX's collectives and lax.ppermute only.
A program may use at most 192 MiB of HBM per device.

```python
import math
import jax
import jax.numpy as jnp
import numpy as np
from jax import lax

D = 4096
FF = 1536
TOP = 8
EXP_DEV = 4
HOT = 6
STEPS = 2
TOK_EP = 128
EXPERTS = 32
TOKENS = 1024
CAP = 40
N_EP = 8


def swap_into(slot_owner, slot_index, expert_id):
    current = jnp.argmax((slot_owner == expert_id).astype(jnp.int32)).astype(jnp.int32)
    displaced = slot_owner[slot_index]
    slot_owner = slot_owner.at[current].set(displaced)
    return slot_owner.at[slot_index].set(expert_id)


def layout(key):
    base_key = jax.random.fold_in(key, 7)
    key_perm, key_device, key_local = jax.random.split(base_key, 3)
    slot_owner = jax.random.permutation(key_perm, EXPERTS).astype(jnp.int32)
    hot_device = jax.random.permutation(key_device, N_EP)[:HOT].astype(jnp.int32)
    hot_local = jax.random.randint(key_local, (HOT,), 0, EXP_DEV).astype(jnp.int32)
    hot_slot = (hot_device * EXP_DEV + hot_local).astype(jnp.int32)
    slot_owner = swap_into(slot_owner, hot_slot[0], jnp.int32(EXPERTS - 1))
    slot_owner = swap_into(slot_owner, hot_slot[1], jnp.int32(0))
    slot_iota = jnp.arange(EXPERTS, dtype=jnp.int32)
    home_table = jnp.zeros((EXPERTS,), jnp.int32).at[slot_owner].set(slot_iota)
    hot_expert = slot_owner[hot_slot]
    device_iota = jnp.arange(N_EP, dtype=jnp.int32)
    chosen = device_iota % HOT
    chosen = jnp.where(hot_device[chosen] == device_iota, (chosen + 1) % HOT, chosen)
    return (home_table, hot_expert[chosen].astype(jnp.int32))


def draw_home_slot(key, part):
    return layout(key)[0]


def draw_spare_expert(key, part):
    return layout(key)[1]


def block_scale(rng, extent, pieces, low, largest):
    gain, own = 1.0, jax.random.fold_in(rng, 6)
    for dim, blocks in pieces:
        heights = jnp.exp(jax.random.uniform(jax.random.fold_in(own, dim), (blocks,), jnp.float32, low / len(pieces), largest / len(pieces)))
        gain = gain * jnp.repeat(heights, extent[dim] // blocks).reshape([-1 if axis == dim else 1 for axis in range(len(extent))])
    return gain


def deal_out(rng, own, number, rows, number_of, top, limit, lean):
    order = jax.random.permutation(rng, number_of)
    packed, usual = shares(number_of, rows * top, limit, lean, True), shares(number_of, rows * top, limit, lean, False)
    places = jnp.arange(number_of)

    def named(sizes, offset_by):
        used = int((sizes > 0).sum())
        fixed = max(1, used // 4)
        passed = fixed + (places - fixed + offset_by * (used - fixed)) % max(1, number_of - fixed)
        return jnp.zeros((number_of,), jnp.int32).at[order[jnp.where(places < fixed, places, passed)]].set(jnp.asarray(sizes, jnp.int32))

    sizes = jnp.where(number % 4 == 0, named(packed, number // 4), named(usual, number - number // 4 - 1))
    mixed = jax.random.permutation(jax.random.fold_in(own, 3), number_of)
    source_of, taker = mixed[0:number_of // 2 * 2:2], mixed[1:number_of // 2 * 2:2]
    margin = jnp.minimum(sizes[source_of] - 1, limit - sizes[taker]) // 2
    margin = jnp.where((source_of == order[0]) | (taker == order[0]) | (sizes[taker] == 0), 0, jnp.maximum(margin, 0))
    passed = jax.random.randint(jax.random.fold_in(own, 4), (number_of // 2,), 0, 1 << 20) % (margin + 1)
    sizes = sizes.at[source_of].add(-passed).at[taker].add(passed)
    labels = jnp.searchsorted(jnp.cumsum(sizes), jnp.arange(rows * top), side="right").astype(jnp.int32)
    grid = labels.reshape(top, rows).T
    grid = grid[jax.random.permutation(jax.random.fold_in(own, 1), rows)]
    offset_by = jax.random.randint(jax.random.fold_in(own, 2), (rows, 1), 0, top)
    return jnp.take_along_axis(grid, (jnp.arange(top)[None, :] + offset_by) % top, axis=1)


def shares(count, total, limit, lean, full):
    weights = [(1 << 20) // math.isqrt(standing ** lean) + 1 for standing in range(1, count + 1)]
    largest = limit if full else min(limit, max(-(-total // count), total * weights[0] // sum(weights)))
    least = 1 if total - largest >= count - 1 else 0
    given, spare = [largest] + [least] * (count - 1), total - largest - least * (count - 1)
    while spare > 0:
        candidates = [i for i in range(1, count) if given[i] < largest] or [i for i in range(1, count) if given[i] < limit]
        whole, remaining = sum([weights[i] for i in candidates]), spare
        for i in candidates:
            more = min(limit - given[i], max(1, remaining * weights[i] // whole), spare)
            given[i] = given[i] + more
            spare = spare - more
    return np.array(given)


def normal_values(own_key, dims, width, bound, cuts=(), kind=jnp.bfloat16):
    gain = block_scale(own_key, dims, cuts, -0.22, 0.18) if cuts else 1.0
    result = jax.random.normal(own_key, dims, jnp.float32) * width * gain
    return jnp.minimum(jnp.maximum(result, -bound), bound).astype(kind)


def setup_inputs(seed: int = 0) -> dict:
    streams_of = jax.random.split(jax.random.key(seed), 9)
    tokens = normal_values(streams_of[0], (STEPS, TOKENS, D), 1.0, 6.0, ((1, 8), (2, 4)))
    expert_ids_keys = jax.random.split(jax.random.fold_in(streams_of[1], 1), STEPS * TOKENS // TOK_EP)
    expert_ids_turns = jax.random.permutation(jax.random.fold_in(streams_of[1], 3), STEPS * TOKENS // TOK_EP)
    expert_ids = jax.vmap(lambda own, number: deal_out(jax.random.fold_in(streams_of[1], 2), own, number, TOK_EP, EXPERTS, TOP, CAP, 1))(expert_ids_keys, expert_ids_turns).reshape((STEPS, TOKENS, TOP))
    route_weight = jnp.clip(jnp.exp(math.log(1.0) - 2.3025851 * jax.random.uniform(streams_of[2], (STEPS, TOKENS, TOP), jnp.float32) ** block_scale(streams_of[2], (STEPS, TOKENS, TOP), ((1, 8),), -0.2, 0.2)), 0.1, 1.0)
    gate_weight = normal_values(streams_of[3], (EXPERTS, FF, D), D ** -0.5, 0.09375, ((0, 8), (1, 4)))
    up_weight = normal_values(streams_of[4], (EXPERTS, FF, D), D ** -0.5, 0.09375, ((0, 8), (1, 4)))
    down_weight = normal_values(streams_of[5], (EXPERTS, FF, D), FF ** -0.5, 0.15625, ((0, 8), (2, 4)))
    home_slot = draw_home_slot(jax.random.fold_in(streams_of[8], 71), 0)
    spare_expert = draw_spare_expert(jax.random.fold_in(streams_of[8], 71), 0)
    return {"tokens": tokens, "expert_ids": expert_ids, "route_weight": route_weight, "gate_weight": gate_weight, "up_weight": up_weight, "down_weight": down_weight, "home_slot": home_slot, "spare_expert": spare_expert}


def reference(tokens, expert_ids, route_weight, gate_weight, up_weight, down_weight, home_slot, spare_expert):
    flat_tokens = tokens.reshape(STEPS * TOKENS, D)
    pair_slot = home_slot[expert_ids.reshape(-1)].astype(jnp.int32)
    pair_weight = route_weight.reshape(-1)
    pair_owner = jnp.arange(STEPS * TOKENS * TOP, dtype=jnp.int32) // TOP
    row_limit = min(CAP * STEPS * N_EP, STEPS * TOKENS * TOP)

    def one_slot(running, slot_id):
        matched = pair_slot == slot_id
        ordering = jnp.argsort(jnp.where(matched, 0, 1).astype(jnp.int32), stable=True)[:row_limit]
        valid = matched[ordering]
        owners = pair_owner[ordering]
        picked = flat_tokens[owners]
        gate_proj = jnp.dot(picked, gate_weight[slot_id].T, preferred_element_type=jnp.float32)
        up_proj = jnp.dot(picked, up_weight[slot_id].T, preferred_element_type=jnp.float32)
        hidden = (jax.nn.silu(gate_proj) * up_proj).astype(jnp.bfloat16)
        expert_out = jnp.dot(hidden, down_weight[slot_id], preferred_element_type=jnp.float32).astype(jnp.bfloat16)
        scale = jnp.where(valid, pair_weight[ordering], jnp.float32(0.0))
        running = running.at[owners].add(expert_out.astype(jnp.float32) * scale[:, None])
        return running, None

    running, unused = lax.scan(one_slot, jnp.zeros((STEPS * TOKENS, D), jnp.float32), jnp.arange(EXPERTS, dtype=jnp.int32))
    mixed = running.reshape(STEPS, TOKENS, D).astype(jnp.bfloat16)
    spare_slot = home_slot[spare_expert].astype(jnp.int32)
    return mixed, gate_weight[spare_slot], up_weight[spare_slot], down_weight[spare_slot]
```

```python
import functools
import math

import jax
import jax.numpy as jnp
from jax import lax
from jax.experimental import pallas as pl
from jax.experimental.pallas import tpu as pltpu
from jax.sharding import PartitionSpec as P

TOP = 8
PACK = 16


def hidden_kernel(tp, group, cap, pos_ref, x_ref, gate_ref, up_ref, out_ref, rows_ref):
    local = rows_ref.shape[0]
    width = x_ref.shape[3]
    block = group * cap
    tall = group * x_ref.shape[2]

    @pl.when(pl.program_id(0) == 0)
    def _():
        def gather(p, carry):
            rows = lax.broadcasted_iota(jnp.int32, (block, tall), 0)
            picks = jnp.concatenate(
                [
                    jnp.where(rows == pos_ref[0, p, e : e + 1, :], 1.0, 0.0).astype(jnp.bfloat16)
                    for e in range(local)
                ],
                axis=0,
            )
            start = pl.multiple_of(p * block, PACK)
            for t in range(tp):
                part = jnp.concatenate(
                    [x_ref[(p * group + j) * tp + t, 0] for j in range(group)], axis=0
                )
                got = jnp.dot(picks, part, preferred_element_type=jnp.float32).astype(jnp.bfloat16)
                for e in range(local):
                    rows_ref[e, pl.ds(start, block), t * width : (t + 1) * width] = got[
                        e * block : (e + 1) * block
                    ]
            return carry

        lax.fori_loop(0, pos_ref.shape[1], gather, 0)

    rows = rows_ref[pl.program_id(0)]
    dims = (((1,), (1,)), ((), ()))
    gate = lax.dot_general(rows, gate_ref[0], dims, preferred_element_type=jnp.float32)
    up = lax.dot_general(rows, up_ref[0], dims, preferred_element_type=jnp.float32)
    out_ref[0] = (gate / (1.0 + jnp.exp(-gate)) * up).astype(out_ref.dtype)


def hidden_units(step, pos, x, gate_weight, up_weight, tp, group, cap):
    local, units, width = gate_weight.shape
    parts, tall = pos.shape[1], pos.shape[3]
    rows = parts * group * cap
    return pl.pallas_call(
        functools.partial(hidden_kernel, tp, group, cap),
        grid=(local,),
        in_specs=[
            pl.BlockSpec((1, parts, local, tall), lambda e: (step, 0, 0, 0)),
            pl.BlockSpec(
                (x.shape[0], 1) + x.shape[2:],
                lambda e: (0, step, 0, 0),
                pipeline_mode=pl.Buffered(1),
            ),
            pl.BlockSpec((1, units, width), lambda e: (e, 0, 0)),
            pl.BlockSpec((1, units, width), lambda e: (e, 0, 0)),
        ],
        out_specs=pl.BlockSpec((1, rows, units), lambda e: (e, 0, 0)),
        out_shape=jax.ShapeDtypeStruct((local, rows, units), jnp.bfloat16),
        scratch_shapes=[pltpu.VMEM((local, rows, width), jnp.bfloat16)],
        compiler_params=pltpu.CompilerParams(vmem_limit_bytes=56 << 20),
        cost_estimate=pl.CostEstimate(
            flops=4 * local * rows * units * width,
            bytes_accessed=4 * local * units * width + 2 * x.size // x.shape[1],
            transcendentals=local * rows * units,
        ),
        name="hidden_units",
    )(pos, x, gate_weight, up_weight)


def combine_kernel(tp, group, cap, has_base, pos_ref, weight_ref, h_ref, down_ref, *refs):
    out_ref, total_ref = refs[1:] if has_base else refs
    expert = pl.program_id(0)
    block = group * cap
    parts, tall, local = pos_ref.shape[1:]
    tokens = tall // group
    h = jnp.concatenate([h_ref[t, 0] for t in range(tp)], axis=1)
    res = jnp.dot(h, down_ref[0], preferred_element_type=jnp.float32).astype(jnp.bfloat16)
    own = lax.broadcasted_iota(jnp.int32, (tall, local), 1) == expert
    for p in range(parts):
        place = jnp.sum(jnp.where(own, pos_ref[0, p], 0), axis=1, keepdims=True)
        weight = jnp.sum(jnp.where(own, weight_ref[0, p], 0.0), axis=1, keepdims=True)
        lanes = lax.broadcasted_iota(jnp.int32, (tall, block), 1)
        picks = jnp.where(lanes == place, 1.0, 0.0).astype(jnp.bfloat16)
        got = weight * jnp.dot(
            picks, res[p * block : (p + 1) * block], preferred_element_type=jnp.float32
        )

        @pl.when(expert == 0)
        def _():
            total_ref[p] = got

        @pl.when(expert > 0)
        def _():
            total_ref[p] += got

    @pl.when(expert == local - 1)
    def _():
        for p in range(parts):
            for j in range(group):
                out_ref[p * group + j, 0] = total_ref[p, j * tokens : (j + 1) * tokens].astype(
                    out_ref.dtype
                )


def combine(step, steps, pos, weight, h, down_weight, group, cap, base):
    tp, local, rows, units = h.shape
    parts, tall = pos.shape[1], pos.shape[2]
    width = down_weight.shape[2]
    tokens = tall // group
    out_block = (parts * group, 1, tokens, width)
    operands = [pos, weight, h, down_weight]
    in_specs = [
        pl.BlockSpec((1, parts, tall, local), lambda e: (step, 0, 0, 0)),
        pl.BlockSpec((1, parts, tall, local), lambda e: (step, 0, 0, 0)),
        pl.BlockSpec((tp, 1, rows, units), lambda e: (0, e, 0, 0)),
        pl.BlockSpec((1, tp * units, width), lambda e: (e, 0, 0)),
    ]
    if base is not None:
        operands.append(base)
        in_specs.append(pl.BlockSpec(memory_space=pl.ANY))
    return pl.pallas_call(
        functools.partial(combine_kernel, tp, group, cap, base is not None),
        grid=(local,),
        in_specs=in_specs,
        out_specs=pl.BlockSpec(out_block, lambda e: (0, step, 0, 0)),
        out_shape=jax.ShapeDtypeStruct((parts * group, steps, tokens, width), jnp.bfloat16),
        scratch_shapes=[pltpu.VMEM((parts, tall, width), jnp.float32)],
        input_output_aliases={} if base is None else {4: 0},
        compiler_params=pltpu.CompilerParams(vmem_limit_bytes=56 << 20),
        cost_estimate=pl.CostEstimate(
            flops=2 * local * rows * tp * units * width,
            bytes_accessed=2 * local * tp * units * width + 2 * h.size,
            transcendentals=0,
        ),
        name="combine",
    )(*operands)


def placing(expert_ids, route_weight, home_slot, local, cap, group):
    experts_all = home_slot.shape[0]
    packed = jnp.concatenate([expert_ids.astype(jnp.float32), route_weight], axis=-1)
    packed = lax.all_gather(packed, "ep")
    ids = packed[..., : expert_ids.shape[-1]].astype(jnp.int32)
    weights = packed[..., expert_ids.shape[-1] :]
    slots = lax.axis_index("ep") * local + lax.iota(jnp.int32, local)
    named = jnp.sum(
        jnp.where(home_slot[None, :] == slots[:, None], lax.iota(jnp.int32, experts_all), 0), axis=1
    )
    match = ids[..., None] == named
    member = jnp.any(match, axis=3)
    weight = jnp.sum(jnp.where(match, weights[..., None], 0.0), axis=3)
    tokens = ids.shape[2]
    earlier = (lax.iota(jnp.int32, tokens)[None, :] < lax.iota(jnp.int32, tokens)[:, None]).astype(
        jnp.bfloat16
    )
    position = jnp.einsum(
        "ut,sbte->sbue", earlier, member.astype(jnp.bfloat16), preferred_element_type=jnp.float32
    ).astype(jnp.int32)
    offset = (lax.iota(jnp.int32, ids.shape[0]) % group * cap)[:, None, None, None]
    position = jnp.where(member, position + offset, -1)
    sources, steps = ids.shape[:2]

    def arrange(v):
        v = v.reshape(sources // group, group, steps, tokens, local)
        return v.transpose(2, 0, 1, 3, 4).reshape(steps, sources // group, group * tokens, local)

    position = arrange(position)
    return position, position.transpose(0, 1, 3, 2), arrange(weight)


def run_steps(tokens, expert_ids, route_weight, gate_weight, up_weight, down_weight, home_slot, tp):
    steps, tok_count = tokens.shape[:2]
    local = gate_weight.shape[0]
    experts_all = home_slot.shape[0]
    cap = tok_count * TOP * 5 // (4 * experts_all)
    group = PACK // math.gcd(PACK, cap)
    x = lax.all_gather(tokens, ("ep", "tp"))
    columns, rows, weight = placing(expert_ids, route_weight, home_slot, local, cap, group)
    out = None
    for step in range(steps):
        h = hidden_units(step, rows, x, gate_weight, up_weight, tp, group, cap)
        h = lax.all_gather(h, "tp")
        out = combine(step, steps, columns, weight, h, down_weight, group, cap, out)
    mixed = lax.psum_scatter(out, "ep", scatter_dimension=0, tiled=True)
    return mixed.reshape(tokens.shape)


def move_spares(gate_weight, up_weight, down_weight, home_slot, spare_expert):
    local_count = gate_weight.shape[0]
    experts_all = home_slot.shape[0]
    owners = spare_expert.shape[0]
    own_index = lax.axis_index("ep")
    expert_iota = lax.iota(jnp.int32, experts_all)
    spare_slot = jnp.sum(jnp.where(spare_expert[:, None] == expert_iota, home_slot, 0), axis=1)
    spare_home = spare_slot // local_count
    own_slot = jnp.max(jnp.where(spare_home == own_index, spare_slot % local_count, 0))
    gate_part = lax.dynamic_index_in_dim(gate_weight, own_slot, 0, keepdims=False)
    up_part = lax.dynamic_index_in_dim(up_weight, own_slot, 0, keepdims=False)
    down_part = lax.dynamic_index_in_dim(down_weight, own_slot, 0, keepdims=False)
    gate_pieces = gate_part.reshape(gate_part.shape[0], owners, gate_part.shape[1] // owners)
    up_pieces = up_part.reshape(up_part.shape[0], owners, up_part.shape[1] // owners)
    down_pieces = down_part.reshape(down_part.shape[0], owners, down_part.shape[1] // owners)
    spread_gate, spread_up, spread_down = (
        lax.all_to_all(gate_pieces, "ep", split_axis=1, concat_axis=1, tiled=True),
        lax.all_to_all(up_pieces, "ep", split_axis=1, concat_axis=1, tiled=True),
        lax.all_to_all(down_pieces, "ep", split_axis=1, concat_axis=1, tiled=True),
    )
    chosen_gate = jnp.take(spread_gate, spare_home, axis=1)
    chosen_up = jnp.take(spread_up, spare_home, axis=1)
    chosen_down = jnp.take(spread_down, spare_home, axis=1)
    landed_gate, landed_up, landed_down = (
        lax.all_to_all(chosen_gate, "ep", split_axis=1, concat_axis=1, tiled=True),
        lax.all_to_all(chosen_up, "ep", split_axis=1, concat_axis=1, tiled=True),
        lax.all_to_all(chosen_down, "ep", split_axis=1, concat_axis=1, tiled=True),
    )
    spare_gate = landed_gate.reshape(1, gate_part.shape[0], gate_part.shape[1])
    spare_up = landed_up.reshape(1, up_part.shape[0], up_part.shape[1])
    spare_down = landed_down.reshape(1, down_part.shape[0], down_part.shape[1])
    return (spare_gate, spare_up, spare_down)


def shards(
    tp, tokens, expert_ids, route_weight, gate_weight, up_weight, down_weight, home_slot, spare_expert
):
    spare_gate, spare_up, spare_down = move_spares(
        gate_weight, up_weight, down_weight, home_slot, spare_expert
    )
    mixed = run_steps(
        tokens, expert_ids, route_weight, gate_weight, up_weight, down_weight, home_slot, tp
    )
    return (mixed, spare_gate, spare_up, spare_down)


def solution(mesh):
    placed = (
        P(None, "ep", "tp"),
        P(None, "ep", None),
        P(None, "ep", None),
        P("ep", "tp", None),
        P("ep", "tp", None),
        P("ep", None, "tp"),
        P(),
        P(),
    )
    return jax.shard_map(
        functools.partial(shards, mesh.shape["tp"]),
        mesh=mesh,
        in_specs=placed,
        out_specs=(
            P(None, "ep", "tp"),
            P("ep", "tp", None),
            P("ep", "tp", None),
            P("ep", None, "tp"),
        ),
        check_vma=False,
    )
```
